32 devices in a mesh: src: 4 (over y, core), tgt: 8 (over z, x).
Axes of the slice: x: 2, y: 2, z: 4, core: 2. Of those that a mesh axis runs over, the one named last changes fastest.
Arguments:
- kernel: bfloat16 [32768, 8192], P('tgt', 'src'), may hold values from -6 to 6
- probes: bfloat16 [3, 64, 8192], P(None, None, 'src'), may hold values from -6 to 6
Outputs:
- middle_basis: float32 [4, 64, 32768], P('src', None, 'tgt')
- coarse_basis: float32 [4, 64, 8, 4096], P(None, None, 'tgt', 'src')
The draws below stay inside these ranges and needn't reach their ends.
All inputs are finite; a program needn't handle non-finite values.
Results may differ from the reference program's by a relative error of at most 0.0003.
Values sent between devices are 32-bit elements; how exact they have to be, the bound alone decides.
A program may use at most 64 MiB of HBM per device.

```python
import math
import jax
import jax.numpy as jnp
from jax import lax

R = 64
ROWS = 4096
COLS = 2048
TROWS = 32768
SCOLS = 8192
N_SRC = 4
N_TGT = 8


def shard_levels(own_key, shape, split, least, top_value):
    def one(position, parts):
        heights = jax.random.uniform(jax.random.fold_in(jax.random.fold_in(own_key, 6), position), (parts,), jnp.float32, least / len(split), top_value / len(split))
        return jnp.repeat(jnp.exp(heights), shape[position] // parts).reshape((-1,) + (1,) * (len(shape) - position - 1))

    loudness = one(*split[0])
    for cut in split[1:]:
        loudness = loudness * one(*cut)
    return loudness


def centred(key, extent, spread, bound, pieces=(), held_as=jnp.bfloat16):
    values = jax.random.normal(key, extent, jnp.float32) * spread
    if len(pieces) > 0:
        values = shard_levels(key, extent, pieces, -0.22, 0.18) * values
    return jnp.clip(values, min=-bound, max=bound).astype(held_as)


def setup_inputs(seed: int = 0) -> dict:
    seeds = jax.random.split(jax.random.key(seed), 3)
    return {
        "kernel": centred(seeds[0], (TROWS, SCOLS), 1.0, 6.0, ((0, 8), (1, 4))),
        "probes": centred(seeds[1], (3, R, SCOLS), 1.0, 6.0, ((2, 4),)),
    }


highest = lax.Precision.HIGHEST

def cross_products(left, right):
    return jnp.einsum('...rm,...sm->...rs', left, right, precision=highest)

def combine_rows(weights, basis):
    return jnp.einsum('...rs,...sm->...rm', weights, basis, precision=highest)

def orthonormal(values, gram):
    factor = jnp.linalg.cholesky(gram)
    return jax.scipy.linalg.solve_triangular(factor, values, lower=True)

def complement(values, basis):
    coefficient = cross_products(values, basis)
    remainder = values - combine_rows(coefficient, basis)
    return orthonormal(remainder, cross_products(remainder, remainder))

def reference(kernel, probes):
    blocks = jnp.arange(N_SRC, dtype=jnp.int32)

    def sketch(level):

        def one_block(index):
            start = (index * COLS).astype(jnp.int32)
            columns = lax.dynamic_slice_in_dim(kernel, start, COLS, 1)
            probe = lax.dynamic_slice_in_dim(probes[level], start, COLS, 1)
            return lax.dot_general(probe.astype(jnp.float32), columns.astype(jnp.float32), (((1,), (1,)), ((), ())), preferred_element_type=jnp.float32)
        return lax.map(one_block, blocks)
    first = sketch(0)
    fine = orthonormal(first, cross_products(first, first))
    second = sketch(1)
    paired = second.reshape(N_SRC // 2, 2, R, TROWS).sum(axis=1)
    pair_sum = jnp.repeat(paired, 2, axis=0)
    middle = complement(pair_sum, fine)
    third = sketch(2)
    grouped = third.reshape(N_SRC // 4, 4, R, TROWS).sum(axis=1)
    group_sum = jnp.repeat(grouped, 4, axis=0)
    coarse = complement(group_sum, jnp.concatenate((fine, middle), axis=1))
    scale = math.sqrt(TROWS)
    return (middle * scale, (coarse * scale).reshape(N_SRC, R, N_TGT, ROWS))
```

```python
import math

import jax
import jax.numpy as jnp
from jax import lax
from jax.sharding import PartitionSpec as P

highest = lax.Precision.HIGHEST


def from_partner(value, axis, stride):
    mask = 2**stride
    pairs = [(source, source ^ mask) for source in range(lax.axis_size(axis))]
    return lax.ppermute(value, axis, pairs)


def to_targets(local_coarse):
    return lax.all_to_all(local_coarse[None], "src", split_axis=2, concat_axis=0, tiled=True)


def shards(kernel, probes):
    count_tgt = lax.axis_size("tgt")
    scale = math.sqrt(kernel.shape[0] * count_tgt)
    levels, rank, cols = probes.shape
    sketch = lax.dot_general(
        probes.reshape(levels * rank, cols), kernel, (((1,), (1,)), ((), ())),
        preferred_element_type=jnp.float32,
    )
    first, second, third = sketch[:rank], sketch[rank:2 * rank], sketch[2 * rank:]
    shared = sketch[rank:]
    shared = shared + from_partner(shared, "src", 0)
    pair_sum = shared[:rank]
    group_sum = shared[rank:]
    group_sum = group_sum + from_partner(group_sum, "src", 1)
    stack = jnp.concatenate((first, pair_sum, group_sum), axis=0)
    gram = lax.psum(jnp.einsum("rm,sm->rs", stack, stack, precision=highest), "tgt")
    factor = jnp.linalg.cholesky(gram)
    inverse = lax.linalg.triangular_solve(factor, jnp.eye(levels * rank, dtype=jnp.float32), left_side=True, lower=True)
    weights = inverse[rank:] * scale
    bases = jnp.einsum("rs,sm->rm", weights, stack, precision=highest)
    coarse = to_targets(bases[rank:])
    return (bases[:rank][None], coarse[:, :, None, :])


def solution(mesh):
    placed = (P("tgt", "src"), P(None, None, "src"))
    return jax.shard_map(
        shards,
        mesh=mesh,
        in_specs=placed,
        out_specs=(P("src", None, "tgt"), P(None, None, "tgt", "src")),
        check_vma=False,
    )
```

```python
import functools
import math

import jax
import jax.numpy as jnp
from jax import lax
from jax.experimental import pallas as pl
from jax.experimental.pallas import tpu as pltpu
from jax.sharding import PartitionSpec as P

highest = lax.Precision.HIGHEST
MESH = pl.DeviceIdType.MESH
LAG_SHARE, LAG_GROUP, LAG_GRAM = 1, 3, 4


def nt_dot(a, b):
    return lax.dot_general(a, b, (((1,), (1,)), ((), ())), preferred_element_type=jnp.float32)


def split(value):
    high = value.astype(jnp.bfloat16)
    return high, (value - high.astype(jnp.float32)).astype(jnp.bfloat16)


def gather_kernel(n_src, n_tgt, tiles, tile, slots, rank,
                  kernel_hbm, probes_ref, stack_out, gram_out,
                  held, own, shared, stack, chip, total, cross, parts, pieces, summed, full,
                  k_sem, o_sem, a_send, a_recv, b_send, b_recv, c_send, c_recv,
                  r_send, r_recv, g_send, g_recv):
    s = lax.axis_index("src")
    t = lax.axis_index("tgt")
    core = lax.rem(s, 2)
    mate = s + 1 - 2 * core
    pair = lax.rem(s // 2, 2)
    across = s + 2 - 4 * pair
    half = rank // 2

    def fetch(i):
        slot = lax.rem(i, slots)
        return pltpu.make_async_copy(
            kernel_hbm.at[pl.ds(pl.multiple_of(i * tile, tile), tile)], held.at[slot], k_sem.at[slot])

    for i in range(min(slots, tiles)):
        fetch(i).start()

    barrier = pltpu.get_barrier_semaphore()
    pl.semaphore_signal(barrier, inc=1, device_id={"src": mate}, device_id_type=MESH)
    pl.semaphore_signal(barrier, inc=1, device_id={"src": across}, device_id_type=MESH)
    for d in range(1, n_tgt):
        pl.semaphore_signal(barrier, inc=1, device_id={"tgt": lax.rem(t + d, n_tgt)}, device_id_type=MESH)
    pl.semaphore_wait(barrier, n_tgt + 1)

    mine = pl.multiple_of(half * core, half)
    theirs = pl.multiple_of(half * (1 - core), half)

    def remote(src, dst, send, recv, device):
        return pltpu.make_async_remote_copy(
            src_ref=src, dst_ref=dst, send_sem=send, recv_sem=recv, device_id=device, device_id_type=MESH)

    def share_pair(j):
        return remote(own.at[j, pl.ds(rank, rank)], shared.at[j, pl.ds(0, rank)],
                      a_send.at[0, j], a_recv.at[0, j], {"src": mate})

    def share_group(j):
        return remote(own.at[j, pl.ds(2 * rank + theirs, half)], shared.at[j, pl.ds(rank, half)],
                      a_send.at[1, j], a_recv.at[1, j], {"src": mate})

    def cross_chip(j):
        return remote(chip.at[0, j], chip.at[1, j], b_send.at[j], b_recv.at[j], {"src": across})

    def hand_over(j):
        return remote(chip.at[2, j], stack.at[j, pl.ds(2 * rank + mine, half)],
                      c_send.at[j], c_recv.at[j], {"src": mate})

    total[...] = jnp.zeros_like(total)
    cross[...] = jnp.zeros_like(cross)

    def step(i, carry):
        @pl.when(i < tiles)
        def _():
            fetch(i).wait()
            own[i] = nt_dot(probes_ref[...], held[lax.rem(i, slots)])
            share_group(i).start()
            share_pair(i).start()

            @pl.when(i + slots < tiles)
            def _():
                fetch(i + slots).start()

        @pl.when((i >= LAG_SHARE) & (i < tiles + LAG_SHARE))
        def _():
            j = i - LAG_SHARE
            share_group(j).wait_recv()
            chip[0, j] = own[j, pl.ds(2 * rank + mine, half)] + shared[j, rank:rank + half]
            cross_chip(j).start()
            share_pair(j).wait_recv()
            stack[j, 0:rank] = own[j, 0:rank]
            stack[j, rank:2 * rank] = own[j, rank:2 * rank] + shared[j, 0:rank]

        @pl.when((i >= LAG_GROUP) & (i < tiles + LAG_GROUP))
        def _():
            j = i - LAG_GROUP
            cross_chip(j).wait_recv()
            value = chip[0, j] + chip[1, j]
            chip[2, j] = value
            stack[j, pl.ds(2 * rank + mine, half)] = value
            hand_over(j).start()

        @pl.when(i >= LAG_GRAM)
        def _():
            j = i - LAG_GRAM
            hand_over(j).wait_recv()
            high, low = split(stack[j])
            total[...] += nt_dot(high, high)
            cross[...] += nt_dot(high, low)
            pltpu.make_async_copy(stack.at[j], stack_out.at[j], o_sem.at[j]).start()

        return carry

    lax.fori_loop(0, tiles + LAG_GRAM, step, 0)

    mixed = cross[...]
    gram = total[...] + (mixed + mixed.T)
    rows = gram.shape[0] // n_tgt
    for p in range(n_tgt):
        parts[p] = gram[p * rows:(p + 1) * rows]

    scatter = []
    for d in range(1, n_tgt):
        to = lax.rem(t + d, n_tgt)
        scatter.append(remote(parts.at[to], pieces.at[d - 1], r_send.at[d - 1], r_recv.at[d - 1], {"tgt": to}))
        scatter[-1].start()
    value = parts[t]
    for d in range(1, n_tgt):
        scatter[d - 1].wait_recv()
        value = value + pieces[d - 1]
    summed[...] = value
    full[t] = value
    gather = []
    for d in range(1, n_tgt):
        to = lax.rem(t + d, n_tgt)
        gather.append(remote(summed, full.at[t], g_send.at[d - 1], g_recv.at[d - 1], {"tgt": to}))
        gather[-1].start()
    for d in range(1, n_tgt):
        origin = lax.rem(t + n_tgt - d, n_tgt)
        remote(summed, full.at[origin], g_send.at[d - 1], g_recv.at[d - 1], {"tgt": origin}).wait_recv()
    for p in range(n_tgt):
        gram_out[p * rows:(p + 1) * rows, :] = full[p]
    for d in range(1, n_tgt):
        scatter[d - 1].wait_send()
        gather[d - 1].wait_send()

    def finish(j, carry):
        share_group(j).wait_send()
        share_pair(j).wait_send()
        cross_chip(j).wait_send()
        hand_over(j).wait_send()
        pltpu.make_async_copy(stack.at[j], stack_out.at[j], o_sem.at[j]).wait()
        return carry

    lax.fori_loop(0, tiles, finish, 0)


def gather(kernel, probes, tile):
    n_src, n_tgt = lax.axis_size("src"), lax.axis_size("tgt")
    rows, cols = kernel.shape
    total_rank = probes.shape[0]
    rank = total_rank // 3
    tiles = rows // tile
    slots = min(4, tiles)
    f32 = jnp.float32
    dma = pltpu.SemaphoreType.DMA
    return pl.pallas_call(
        functools.partial(gather_kernel, n_src, n_tgt, tiles, tile, slots, rank),
        out_shape=(jax.ShapeDtypeStruct((tiles, total_rank, tile), f32),
                   jax.ShapeDtypeStruct((total_rank, total_rank), f32)),
        in_specs=[pl.BlockSpec(memory_space=pl.ANY), pl.BlockSpec(memory_space=pltpu.VMEM)],
        out_specs=(pl.BlockSpec(memory_space=pl.ANY), pl.BlockSpec(memory_space=pltpu.VMEM)),
        scratch_shapes=[
            pltpu.VMEM((slots, tile, cols), kernel.dtype),
            pltpu.VMEM((tiles, total_rank, tile), f32),
            pltpu.VMEM((tiles, rank + rank // 2, tile), f32),
            pltpu.VMEM((tiles, total_rank, tile), f32),
            pltpu.VMEM((3, tiles, rank // 2, tile), f32),
            pltpu.VMEM((total_rank, total_rank), f32),
            pltpu.VMEM((total_rank, total_rank), f32),
            pltpu.VMEM((n_tgt, total_rank // n_tgt, total_rank), f32),
            pltpu.VMEM((n_tgt - 1, total_rank // n_tgt, total_rank), f32),
            pltpu.VMEM((total_rank // n_tgt, total_rank), f32),
            pltpu.VMEM((n_tgt, total_rank // n_tgt, total_rank), f32),
            dma((slots,)), dma((tiles,)),
            dma((2, tiles)), dma((2, tiles)), dma((tiles,)), dma((tiles,)), dma((tiles,)), dma((tiles,)),
            dma((n_tgt - 1,)), dma((n_tgt - 1,)), dma((n_tgt - 1,)), dma((n_tgt - 1,)),
        ],
        compiler_params=pltpu.CompilerParams(collective_id=0, has_side_effects=True),
        name="gather",
    )(kernel, probes)


def inverse_factor(a, chunk=4):
    n = a.shape[0]
    lanes = 2 * n
    m = jnp.concatenate([a, jnp.eye(n, dtype=a.dtype)], axis=1)
    blocks = [m[8 * r:8 * r + 8] for r in range(n // 8)]
    row_ids = lax.broadcasted_iota(jnp.int32, (8, lanes), 0)
    for start in range(0, n, chunk):
        top = start // 8
        cols = [{r: jnp.broadcast_to(blocks[r][:, start + q:start + q + 1], (8, lanes)) for r in range(top, n // 8)}
                for q in range(chunk)]
        for q in range(chunk):
            inner = (start + q) % 8
            pivot = jnp.broadcast_to(cols[q][top][inner:inner + 1], (8, lanes))
            inv = 1.0 / pivot
            row = jnp.broadcast_to(blocks[top][inner:inner + 1], (8, lanes))
            later = [jnp.broadcast_to(cols[p][top][inner:inner + 1], (8, lanes)) for p in range(q + 1, chunk)]
            row = row * inv
            later = [value * inv for value in later]
            for r in range(top, n // 8):
                mult = cols[q][r]
                if r == top:
                    mult = jnp.where(row_ids > inner, mult, 0.0)
                for p in range(q + 1, chunk):
                    cols[p][r] = cols[p][r] - mult * later[p - q - 1]
                blocks[r] = blocks[r] - mult * row
    m = jnp.concatenate(blocks, axis=0)
    r_ids = lax.broadcasted_iota(jnp.int32, (n, lanes), 0)
    c_ids = lax.broadcasted_iota(jnp.int32, (n, lanes), 1)
    pivots = jnp.sum(jnp.where(r_ids == c_ids, m, 0.0), axis=1, keepdims=True)
    return m[:, n:] * (1.0 / jnp.sqrt(pivots))


def mm(a, b):
    return lax.dot_general(a, b, (((1,), (0,)), ((), ())), precision=highest, preferred_element_type=jnp.float32)


def mmt(a, b):
    return lax.dot_general(a, b, (((1,), (1,)), ((), ())), precision=highest, preferred_element_type=jnp.float32)


def weights_kernel(rank, scale, gram_ref, weights_ref):
    x0 = inverse_factor(gram_ref[0:rank, 0:rank])
    c1 = mmt(gram_ref[rank:, 0:rank], x0)
    rest = gram_ref[rank:, rank:] - mmt(c1, c1)
    x1 = inverse_factor(rest[0:rank, 0:rank])
    c2 = mmt(rest[rank:, 0:rank], x1)
    x2 = inverse_factor(rest[rank:, rank:] - mmt(c2, c2))
    c1x0 = mm(c1, x0)
    mid_first = -mm(x1, c1x0[0:rank])
    weights_ref[0:rank, 0:rank] = scale * mid_first
    weights_ref[0:rank, rank:2 * rank] = scale * x1
    weights_ref[0:rank, 2 * rank:] = jnp.zeros_like(x1)
    weights_ref[rank:, 0:rank] = scale * mm(x2, -c1x0[rank:] - mm(c2, mid_first))
    weights_ref[rank:, rank:2 * rank] = -scale * mm(x2, mm(c2, x1))
    weights_ref[rank:, 2 * rank:] = scale * x2


def weights_of(gram, scale):
    total_rank = gram.shape[0]
    rank = total_rank // 3
    return pl.pallas_call(
        functools.partial(weights_kernel, rank, scale),
        out_shape=jax.ShapeDtypeStruct((2 * rank, total_rank), jnp.float32),
        name="weights",
    )(gram)


def spread_kernel(n_src, tiles, tile, rank, weights_ref, stack_hbm, middle_ref, coarse_ref,
                  stack, wsplit, outgoing, k_sem, send, recv):
    s = lax.axis_index("src")
    per = tiles // n_src

    def fetch(j):
        return pltpu.make_async_copy(stack_hbm.at[j], stack.at[j], k_sem.at[j])

    order = [(lax.rem(s + d + 2, n_src), q) for d in range(n_src) for q in range(per)]
    index = [(to * per + q) for to, q in order]
    for j in index:
        fetch(j).start()

    barrier = pltpu.get_barrier_semaphore()
    for d in range(1, n_src):
        pl.semaphore_signal(barrier, inc=1, device_id={"src": lax.rem(s + d, n_src)}, device_id_type=MESH)
    pl.semaphore_wait(barrier, n_src - 1)

    high, low = split(weights_ref[...])
    wsplit[0:2 * rank] = high
    wsplit[2 * rank:] = low

    def product(j):
        shigh, slow = split(stack[j])
        both = jnp.dot(wsplit[...], shigh, preferred_element_type=jnp.float32)
        return both[0:2 * rank] + (both[2 * rank:] + jnp.dot(wsplit[0:2 * rank], slow, preferred_element_type=jnp.float32))

    copies = []
    for d in range(n_src):
        away = (d + 2) % n_src
        to = lax.rem(s + away, n_src)
        for q in range(per):
            j = to * per + q
            fetch(j).wait()
            value = product(j)
            middle_ref[:, pl.ds(pl.multiple_of(j * tile, tile), tile)] = value[0:rank]
            if away == 0:
                coarse_ref[s, :, q * tile:(q + 1) * tile] = value[rank:]
            else:
                outgoing[(away - 1) * per + q] = value[rank:]
                k = (away - 1) * per + q
                copies.append(pltpu.make_async_remote_copy(
                    src_ref=outgoing.at[k], dst_ref=coarse_ref.at[s, :, pl.ds(q * tile, tile)],
                    send_sem=send.at[k], recv_sem=recv.at[k], device_id={"src": to}, device_id_type=MESH))
                copies[-1].start()
    for away in range(1, n_src):
        origin = lax.rem(s + n_src - away, n_src)
        for q in range(per):
            k = (away - 1) * per + q
            pltpu.make_async_remote_copy(
                src_ref=outgoing.at[k], dst_ref=coarse_ref.at[origin, :, pl.ds(q * tile, tile)],
                send_sem=send.at[k], recv_sem=recv.at[k], device_id={"src": origin}, device_id_type=MESH).wait_recv()
    for copy in copies:
        copy.wait_send()


def spread(weights, stack):
    n_src = lax.axis_size("src")
    tiles, total_rank, tile = stack.shape
    rank = total_rank // 3
    f32 = jnp.float32
    moved = (n_src - 1) * (tiles // n_src)
    dma = pltpu.SemaphoreType.DMA
    return pl.pallas_call(
        functools.partial(spread_kernel, n_src, tiles, tile, rank),
        out_shape=(jax.ShapeDtypeStruct((rank, tiles * tile), f32),
                   jax.ShapeDtypeStruct((n_src, rank, tiles * tile // n_src), f32)),
        in_specs=[pl.BlockSpec(memory_space=pltpu.VMEM), pl.BlockSpec(memory_space=pl.ANY)],
        out_specs=(pl.BlockSpec(memory_space=pltpu.VMEM), pl.BlockSpec(memory_space=pltpu.VMEM)),
        scratch_shapes=[
            pltpu.VMEM((tiles, total_rank, tile), f32),
            pltpu.VMEM((4 * rank, total_rank), jnp.bfloat16),
            pltpu.VMEM((moved, rank, tile), f32),
            dma((tiles,)), dma((moved,)), dma((moved,)),
        ],
        compiler_params=pltpu.CompilerParams(collective_id=1, has_side_effects=True),
        name="spread",
    )(weights, stack)


def shards(kernel, probes):
    n_src, n_tgt = lax.axis_size("src"), lax.axis_size("tgt")
    rows = kernel.shape[0]
    scale = math.sqrt(rows * n_tgt)
    levels, rank, cols = probes.shape
    tile = min(512, rows // n_src)
    stack, gram = gather(kernel, probes.reshape(levels * rank, cols), tile)
    weights = weights_of(gram, scale)
    middle, coarse = spread(weights, stack)
    return (middle[None], coarse[:, :, None, :])


def solution(mesh):
    placed = (P("tgt", "src"), P(None, None, "src"))
    return jax.shard_map(
        shards,
        mesh=mesh,
        in_specs=placed,
        out_specs=(P("src", None, "tgt"), P(None, None, "tgt", "src")),
        check_vma=False,
    )
```

```python
import functools
import math

import jax
import jax.numpy as jnp
from jax import lax
from jax.experimental import pallas as pl
from jax.experimental.pallas import tpu as pltpu
from jax.sharding import PartitionSpec as P

highest = lax.Precision.HIGHEST
MESH = pl.DeviceIdType.MESH


def nt_dot(a, b):
    return lax.dot_general(a, b, (((1,), (1,)), ((), ())), preferred_element_type=jnp.float32)


def split(value):
    high = value.astype(jnp.bfloat16)
    return high, (value - high.astype(jnp.float32)).astype(jnp.bfloat16)


def inverse_factor(a, chunk=4):
    n = a.shape[0]
    lanes = 2 * n
    m = jnp.concatenate([a, jnp.eye(n, dtype=a.dtype)], axis=1)
    blocks = [m[8 * r:8 * r + 8] for r in range(n // 8)]
    row_ids = lax.broadcasted_iota(jnp.int32, (8, lanes), 0)
    for start in range(0, n, chunk):
        top = start // 8
        cols = [{r: jnp.broadcast_to(blocks[r][:, start + q:start + q + 1], (8, lanes)) for r in range(top, n // 8)}
                for q in range(chunk)]
        for q in range(chunk):
            inner = (start + q) % 8
            pivot = jnp.broadcast_to(cols[q][top][inner:inner + 1], (8, lanes))
            inv = 1.0 / pivot
            row = jnp.broadcast_to(blocks[top][inner:inner + 1], (8, lanes))
            later = [jnp.broadcast_to(cols[p][top][inner:inner + 1], (8, lanes)) for p in range(q + 1, chunk)]
            row = row * inv
            later = [value * inv for value in later]
            for r in range(top, n // 8):
                mult = cols[q][r]
                if r == top:
                    mult = jnp.where(row_ids > inner, mult, 0.0)
                for p in range(q + 1, chunk):
                    cols[p][r] = cols[p][r] - mult * later[p - q - 1]
                blocks[r] = blocks[r] - mult * row
    m = jnp.concatenate(blocks, axis=0)
    r_ids = lax.broadcasted_iota(jnp.int32, (n, lanes), 0)
    c_ids = lax.broadcasted_iota(jnp.int32, (n, lanes), 1)
    pivots = jnp.sum(jnp.where(r_ids == c_ids, m, 0.0), axis=1, keepdims=True)
    return m[:, n:] * (1.0 / jnp.sqrt(pivots))


def mm(a, b):
    return lax.dot_general(a, b, (((1,), (0,)), ((), ())), precision=highest, preferred_element_type=jnp.float32)


def mmt(a, b):
    return lax.dot_general(a, b, (((1,), (1,)), ((), ())), precision=highest, preferred_element_type=jnp.float32)


def flip(index, mask):
    result = 0
    place = 1
    while place <= mask:
        bit = lax.rem(index // place, 2)
        result = result + place * ((1 - bit) if mask & place else bit)
        place *= 2
    return result + (index // place) * place


def remote(src, dst, send, recv, device):
    return pltpu.make_async_remote_copy(
        src_ref=src, dst_ref=dst, send_sem=send, recv_sem=recv, device_id=device, device_id_type=MESH)


class Reduction:
    def __init__(self, n, parts, pieces, summed, full, sems):
        self.n, self.parts, self.pieces, self.summed, self.full = n, parts, pieces, summed, full
        self.r_send, self.r_recv, self.g_send, self.g_recv = (sems.at[k] for k in range(4))
        self.t = lax.axis_index("tgt")

    def scatter(self, value):
        rows = value.shape[0] // self.n
        for p in range(self.n):
            self.parts[p] = value[p * rows:(p + 1) * rows]
        self.sent = []
        for d in range(1, self.n):
            to = lax.rem(self.t + d, self.n)
            self.sent.append(remote(self.parts.at[to], self.pieces.at[d - 1],
                                    self.r_send.at[d - 1], self.r_recv.at[d - 1], {"tgt": to}))
            self.sent[-1].start()

    def gather(self):
        value = self.parts[self.t]
        for d in range(1, self.n):
            self.sent[d - 1].wait_recv()
            value = value + self.pieces[d - 1]
        self.summed[...] = value
        self.full[self.t] = value
        for d in range(1, self.n):
            to = lax.rem(self.t + d, self.n)
            self.sent.append(remote(self.summed, self.full.at[self.t],
                                    self.g_send.at[d - 1], self.g_recv.at[d - 1], {"tgt": to}))
            self.sent[-1].start()

    def result(self):
        for d in range(1, self.n):
            origin = lax.rem(self.t + self.n - d, self.n)
            remote(self.summed, self.full.at[origin], self.g_send.at[d - 1], self.g_recv.at[d - 1],
                   {"tgt": origin}).wait_recv()
        return jnp.concatenate([self.full[p] for p in range(self.n)], axis=0)

    def drain(self):
        for copy in self.sent:
            copy.wait_send()


def moved_rows(mask, rank):
    return rank * (3 if mask % 4 == 0 else 2 if mask % 2 == 0 else 1)


def gather_kernel(n_src, n_tgt, tiles, tile, slots, rank, scale,
                  kernel_hbm, probes_ref, stack_out, moved_out, middle_out, coarse_out,
                  held, own, shared, stack, chip, total, cross,
                  parts_a, pieces_a, summed_a, full_a, parts_b, pieces_b, summed_b, full_b,
                  k_sem, o_sem, a_send, a_recv, b_send, b_recv, c_send, c_recv,
                  ra_sems, rb_sems, m_send, m_recv, w_send, w_recv):
    s = lax.axis_index("src")
    t = lax.axis_index("tgt")
    core = lax.rem(s, 2)
    mate = flip(s, 1)
    across = flip(s, 2)
    half = rank // 2
    per = tiles // n_src

    def fetch(i):
        slot = lax.rem(i, slots)
        return pltpu.make_async_copy(
            kernel_hbm.at[pl.ds(pl.multiple_of(i * tile, tile), tile)], held.at[slot], k_sem.at[slot])

    for i in range(min(slots, tiles)):
        fetch(i).start()

    barrier = pltpu.get_barrier_semaphore()
    for mask in range(1, n_src):
        pl.semaphore_signal(barrier, inc=1, device_id={"src": flip(s, mask)}, device_id_type=MESH)
    for d in range(1, n_tgt):
        pl.semaphore_signal(barrier, inc=1, device_id={"tgt": lax.rem(t + d, n_tgt)}, device_id_type=MESH)
    pl.semaphore_wait(barrier, n_tgt + n_src - 2)

    mine = pl.multiple_of(half * core, half)
    theirs = pl.multiple_of(half * (1 - core), half)

    def share_pair(j):
        return remote(own.at[j, pl.ds(rank, rank)], shared.at[j, pl.ds(0, rank)],
                      a_send.at[0, j], a_recv.at[0, j], {"src": mate})

    def share_group(j):
        return remote(own.at[j, pl.ds(2 * rank + theirs, half)], shared.at[j, pl.ds(rank, half)],
                      a_send.at[1, j], a_recv.at[1, j], {"src": mate})

    def cross_chip(j):
        return remote(chip.at[0, j], chip.at[1, j], b_send.at[j], b_recv.at[j], {"src": across})

    def hand_over(j):
        return remote(chip.at[2, j], stack.at[j, pl.ds(2 * rank + mine, half)],
                      c_send.at[j], c_recv.at[j], {"src": mate})

    def move(mask, q):
        to = flip(s, mask)
        count = moved_rows(mask, rank)
        return remote(stack.at[to * per + q, pl.ds(0, count)], moved_out.at[mask - 1, q, pl.ds(0, count)],
                      m_send.at[mask - 1, q], m_recv.at[mask - 1, q], {"src": to})

    def save(j):
        return pltpu.make_async_copy(stack.at[j], stack_out.at[j], o_sem.at[j])

    total[...] = jnp.zeros_like(total)
    cross[...] = jnp.zeros_like(cross)

    def step(i, carry):
        @pl.when(i < tiles)
        def _():
            fetch(i).wait()
            own[i] = nt_dot(probes_ref[...], held[lax.rem(i, slots)])
            share_group(i).start()
            share_pair(i).start()

            @pl.when(i + slots < tiles)
            def _():
                fetch(i + slots).start()

        @pl.when(i >= 1)
        def _():
            j = i - 1
            share_group(j).wait_recv()
            chip[0, j] = own[j, pl.ds(2 * rank + mine, half)] + shared[j, rank:rank + half]
            cross_chip(j).start()
            share_pair(j).wait_recv()
            first = own[j, 0:rank]
            second = own[j, rank:2 * rank] + shared[j, 0:rank]
            both = jnp.concatenate([first, second], axis=0)
            stack[j, 0:2 * rank] = both
            high, low = split(both)
            total[...] += nt_dot(high, high)
            cross[...] += nt_dot(high, low)

        return carry

    lax.fori_loop(0, tiles + 1, step, 0)

    lower = Reduction(n_tgt, parts_a, pieces_a, summed_a, full_a, ra_sems)
    mixed = cross[...]
    lower.scatter(total[...] + (mixed + mixed.T))
    late = []
    for mask in (2, 3, 1) + tuple(range(4, n_src)):
        for q in range(per):
            if mask % 4 == 0:
                late.append((mask, q))
            else:
                move(mask, q).start()

    def group(j, carry):
        cross_chip(j).wait_recv()
        value = chip[0, j] + chip[1, j]
        chip[2, j] = value
        stack[j, pl.ds(2 * rank + mine, half)] = value
        hand_over(j).start()
        return carry

    early = (tiles * 3) // 4
    lax.fori_loop(0, early, group, 0)
    lower.gather()
    lax.fori_loop(early, tiles, group, 0)

    def upper_gram(j, carry):
        hand_over(j).wait_recv()
        save(j).start()
        high, low = split(stack[j])
        top = high[2 * rank:]
        return carry + (nt_dot(top, high) + (nt_dot(top, low) + nt_dot(low[2 * rank:], high)))

    upper_value = lax.fori_loop(0, tiles, upper_gram, jnp.zeros((rank, 3 * rank), jnp.float32))
    for mask, q in late:
        move(mask, q).start()
    upper = Reduction(n_tgt, parts_b, pieces_b, summed_b, full_b, rb_sems)
    upper.scatter(upper_value)

    low_gram = lower.result()
    x0 = inverse_factor(low_gram[0:rank, 0:rank])
    c_pair = mmt(low_gram[rank:, 0:rank], x0)
    rest = low_gram[rank:, rank:] - mmt(c_pair, c_pair)
    upper.gather()
    x1 = inverse_factor(rest)
    mid_first = -mm(x1, mm(c_pair, x0))
    middle_out[:, 0:rank] = scale * mid_first
    middle_out[:, rank:] = scale * x1
    up_gram = upper.result()
    c_first = mmt(up_gram[:, 0:rank], x0)
    c_mid = mmt(up_gram[:, rank:2 * rank] - mmt(c_first, c_pair), x1)
    x2 = inverse_factor(up_gram[:, 2 * rank:] - mmt(c_first, c_first) - mmt(c_mid, c_mid))
    coarse_out[0, :, 0:rank] = -scale * mm(x2, mm(c_first, x0) + mm(c_mid, mid_first))
    coarse_out[0, :, rank:2 * rank] = -scale * mm(x2, mm(c_mid, x1))
    coarse_out[0, :, 2 * rank:] = scale * x2

    def tell(mask):
        return remote(coarse_out.at[0], coarse_out.at[mask], w_send.at[mask - 1], w_recv.at[mask - 1],
                      {"src": flip(s, mask)})

    for mask in range(1, n_src):
        tell(mask).start()

    lower.drain()
    upper.drain()

    def finish(j, carry):
        share_group(j).wait_send()
        share_pair(j).wait_send()
        cross_chip(j).wait_send()
        hand_over(j).wait_send()
        save(j).wait()
        return carry

    lax.fori_loop(0, tiles, finish, 0)
    for mask in range(1, n_src):
        for q in range(per):
            move(mask, q).wait()
    for mask in range(1, n_src):
        tell(mask).wait()


def gather(kernel, probes, tile, scale):
    n_src, n_tgt = lax.axis_size("src"), lax.axis_size("tgt")
    rows, cols = kernel.shape
    total_rank = probes.shape[0]
    rank = total_rank // 3
    tiles = rows // tile
    per = tiles // n_src
    slots = min(4, tiles)
    f32 = jnp.float32
    dma = pltpu.SemaphoreType.DMA
    low, up = 2 * rank, rank
    return pl.pallas_call(
        functools.partial(gather_kernel, n_src, n_tgt, tiles, tile, slots, rank, scale),
        out_shape=(jax.ShapeDtypeStruct((tiles, total_rank, tile), f32),
                   jax.ShapeDtypeStruct((n_src - 1, per, total_rank, tile), f32),
                   jax.ShapeDtypeStruct((rank, 2 * rank), f32),
                   jax.ShapeDtypeStruct((n_src, rank, total_rank), f32)),
        in_specs=[pl.BlockSpec(memory_space=pl.ANY), pl.BlockSpec(memory_space=pltpu.VMEM)],
        out_specs=(pl.BlockSpec(memory_space=pl.ANY), pl.BlockSpec(memory_space=pl.ANY),
                   pl.BlockSpec(memory_space=pltpu.VMEM), pl.BlockSpec(memory_space=pltpu.VMEM)),
        scratch_shapes=[
            pltpu.VMEM((slots, tile, cols), kernel.dtype),
            pltpu.VMEM((tiles, total_rank, tile), f32),
            pltpu.VMEM((tiles, rank + rank // 2, tile), f32),
            pltpu.VMEM((tiles, total_rank, tile), f32),
            pltpu.VMEM((3, tiles, rank // 2, tile), f32),
            pltpu.VMEM((low, low), f32),
            pltpu.VMEM((low, low), f32),
            pltpu.VMEM((n_tgt, low // n_tgt, low), f32),
            pltpu.VMEM((n_tgt - 1, low // n_tgt, low), f32),
            pltpu.VMEM((low // n_tgt, low), f32),
            pltpu.VMEM((n_tgt, low // n_tgt, low), f32),
            pltpu.VMEM((n_tgt, up // n_tgt, total_rank), f32),
            pltpu.VMEM((n_tgt - 1, up // n_tgt, total_rank), f32),
            pltpu.VMEM((up // n_tgt, total_rank), f32),
            pltpu.VMEM((n_tgt, up // n_tgt, total_rank), f32),
            dma((slots,)), dma((tiles,)),
            dma((2, tiles)), dma((2, tiles)), dma((tiles,)), dma((tiles,)), dma((tiles,)), dma((tiles,)),
            dma((4, n_tgt - 1)), dma((4, n_tgt - 1)),
            dma((n_src - 1, per)), dma((n_src - 1, per)), dma((n_src - 1,)), dma((n_src - 1,)),
        ],
        compiler_params=pltpu.CompilerParams(collective_id=0, has_side_effects=True),
        name="gather",
    )(kernel, probes)


def finish_kernel(n_src, tiles, tile, rank, stack_hbm, moved_hbm, middle_w, coarse_w, middle_ref, coarse_ref,
                  stack, moved, mine, s_sem, m_sem, o_sem):
    s = lax.axis_index("src")
    per = tiles // n_src

    def fetch(j):
        return pltpu.make_async_copy(stack_hbm.at[j, pl.ds(0, 2 * rank)], stack.at[j], s_sem.at[j])

    def fetch_mine(q):
        return pltpu.make_async_copy(stack_hbm.at[s * per + q], mine.at[q], o_sem.at[q])

    def fetch_moved(mask, q):
        count = moved_rows(mask, rank)
        return pltpu.make_async_copy(moved_hbm.at[mask - 1, q, pl.ds(0, count)],
                                     moved.at[mask - 1, q, pl.ds(0, count)], m_sem.at[mask - 1, q])

    for q in range(per):
        fetch_mine(q).start()
    for mask in range(1, n_src):
        for q in range(per):
            fetch_moved(mask, q).start()
    for j in range(tiles):
        fetch(j).start()

    def product(weights, operand):
        w_high, w_low = split(weights)
        high, low = split(operand)
        count = weights.shape[0]
        both = jnp.dot(jnp.concatenate([w_high, w_low], axis=0), high, preferred_element_type=jnp.float32)
        return both[:count] + (both[count:] + jnp.dot(w_high, low, preferred_element_type=jnp.float32))

    for q in range(per):
        fetch_mine(q).wait()
    for mask in range(n_src):
        for q in range(per):
            if mask:
                fetch_moved(mask, q).wait()

            def rows(source, index):
                ref = moved.at[source - 1, q] if source else mine.at[q]
                return ref[index * rank:(index + 1) * rank]

            operand = jnp.concatenate(
                [rows(mask, 0), rows(mask - mask % 2, 1), rows(mask - mask % 4, 2)], axis=0)
            coarse_ref[flip(s, mask), :, 0, q * tile:(q + 1) * tile] = product(coarse_w[mask], operand)
    for j in range(tiles):
        fetch(j).wait()
        middle_ref[0, :, j * tile:(j + 1) * tile] = product(middle_w[...], stack[j])


def finish(stack, moved, middle_w, coarse_w):
    n_src = lax.axis_size("src")
    tiles, total_rank, tile = stack.shape
    rank = total_rank // 3
    per = tiles // n_src
    f32 = jnp.float32
    dma = pltpu.SemaphoreType.DMA
    vmem = pl.BlockSpec(memory_space=pltpu.VMEM)
    hbm = pl.BlockSpec(memory_space=pl.ANY)
    return pl.pallas_call(
        functools.partial(finish_kernel, n_src, tiles, tile, rank),
        out_shape=(jax.ShapeDtypeStruct((1, rank, tiles * tile), f32),
                   jax.ShapeDtypeStruct((n_src, rank, 1, per * tile), f32)),
        in_specs=[hbm, hbm, vmem, vmem],
        out_specs=(vmem, vmem),
        scratch_shapes=[
            pltpu.VMEM((tiles, 2 * rank, tile), f32),
            pltpu.VMEM((n_src - 1, per, total_rank, tile), f32),
            pltpu.VMEM((per, total_rank, tile), f32),
            dma((tiles,)), dma((n_src - 1, per)), dma((per,)),
        ],
        name="finish",
    )(stack, moved, middle_w, coarse_w)


def shards(kernel, probes):
    n_src, n_tgt = lax.axis_size("src"), lax.axis_size("tgt")
    rows = kernel.shape[0]
    scale = math.sqrt(rows * n_tgt)
    levels, rank, cols = probes.shape
    tile = min(512, rows // n_src)
    return finish(*gather(kernel, probes.reshape(levels * rank, cols), tile, scale))


def solution(mesh):
    placed = (P("tgt", "src"), P(None, None, "src"))
    return jax.shard_map(
        shards,
        mesh=mesh,
        in_specs=placed,
        out_specs=(P("src", None, "tgt"), P(None, None, "tgt", "src")),
        check_vma=False,
    )
```

```python
import functools
import math

import jax
import jax.numpy as jnp
from jax import lax
from jax.experimental import pallas as pl
from jax.experimental.pallas import tpu as pltpu
from jax.sharding import PartitionSpec as P

highest = lax.Precision.HIGHEST
MESH = pl.DeviceIdType.MESH


def nt_dot(a, b):
    return lax.dot_general(a, b, (((1,), (1,)), ((), ())), preferred_element_type=jnp.float32)


def split(value):
    high = value.astype(jnp.bfloat16)
    return high, (value - high.astype(jnp.float32)).astype(jnp.bfloat16)


def inverse_factor(a, chunk=4):
    n = a.shape[0]
    lanes = 2 * n
    m = jnp.concatenate([a, jnp.eye(n, dtype=a.dtype)], axis=1)
    blocks = [m[8 * r:8 * r + 8] for r in range(n // 8)]
    row_ids = lax.broadcasted_iota(jnp.int32, (8, lanes), 0)
    for start in range(0, n, chunk):
        top = start // 8
        cols = [{r: jnp.broadcast_to(blocks[r][:, start + q:start + q + 1], (8, lanes)) for r in range(top, n // 8)}
                for q in range(chunk)]
        for q in range(chunk):
            inner = (start + q) % 8
            pivot = jnp.broadcast_to(cols[q][top][inner:inner + 1], (8, lanes))
            inv = 1.0 / pivot
            row = jnp.broadcast_to(blocks[top][inner:inner + 1], (8, lanes))
            later = [jnp.broadcast_to(cols[p][top][inner:inner + 1], (8, lanes)) for p in range(q + 1, chunk)]
            row = row * inv
            later = [value * inv for value in later]
            for r in range(top, n // 8):
                mult = cols[q][r]
                if r == top:
                    mult = jnp.where(row_ids > inner, mult, 0.0)
                for p in range(q + 1, chunk):
                    cols[p][r] = cols[p][r] - mult * later[p - q - 1]
                blocks[r] = blocks[r] - mult * row
    m = jnp.concatenate(blocks, axis=0)
    r_ids = lax.broadcasted_iota(jnp.int32, (n, lanes), 0)
    c_ids = lax.broadcasted_iota(jnp.int32, (n, lanes), 1)
    pivots = jnp.sum(jnp.where(r_ids == c_ids, m, 0.0), axis=1, keepdims=True)
    return m[:, n:] * (1.0 / jnp.sqrt(pivots))


def mm(a, b):
    return lax.dot_general(a, b, (((1,), (0,)), ((), ())), precision=highest, preferred_element_type=jnp.float32)


def mmt(a, b):
    return lax.dot_general(a, b, (((1,), (1,)), ((), ())), precision=highest, preferred_element_type=jnp.float32)


def flip(index, mask):
    result = 0
    place = 1
    while place <= mask:
        bit = lax.rem(index // place, 2)
        result = result + place * ((1 - bit) if mask & place else bit)
        place *= 2
    return result + (index // place) * place


def remote(src, dst, send, recv, device):
    return pltpu.make_async_remote_copy(
        src_ref=src, dst_ref=dst, send_sem=send, recv_sem=recv, device_id=device, device_id_type=MESH)


class Reduction:
    def __init__(self, n, parts, pieces, summed, full, sems):
        self.n, self.parts, self.pieces, self.summed, self.full = n, parts, pieces, summed, full
        self.r_send, self.r_recv, self.g_send, self.g_recv = (sems.at[k] for k in range(4))
        self.t = lax.axis_index("tgt")

    def scatter(self, value):
        rows = value.shape[0] // self.n
        for p in range(self.n):
            self.parts[p] = value[p * rows:(p + 1) * rows]
        self.sent = []
        for d in range(1, self.n):
            to = lax.rem(self.t + d, self.n)
            self.sent.append(remote(self.parts.at[to], self.pieces.at[d - 1],
                                    self.r_send.at[d - 1], self.r_recv.at[d - 1], {"tgt": to}))
            self.sent[-1].start()

    def gather(self):
        value = self.parts[self.t]
        for d in range(1, self.n):
            self.sent[d - 1].wait_recv()
            value = value + self.pieces[d - 1]
        self.summed[...] = value
        self.full[self.t] = value
        for d in range(1, self.n):
            to = lax.rem(self.t + d, self.n)
            self.sent.append(remote(self.summed, self.full.at[self.t],
                                    self.g_send.at[d - 1], self.g_recv.at[d - 1], {"tgt": to}))
            self.sent[-1].start()

    def result(self):
        for d in range(1, self.n):
            origin = lax.rem(self.t + self.n - d, self.n)
            remote(self.summed, self.full.at[origin], self.g_send.at[d - 1], self.g_recv.at[d - 1],
                   {"tgt": origin}).wait_recv()
        return jnp.concatenate([self.full[p] for p in range(self.n)], axis=0)

    def drain(self):
        for copy in self.sent:
            copy.wait_send()


def moved_rows(mask, rank):
    return rank * (3 if mask % 4 == 0 else 2 if mask % 2 == 0 else 1)


def gather_kernel(n_src, n_tgt, tiles, tile, slots, rank, scale,
                  kernel_hbm, probes_ref, stack_out, moved_out, middle_out, coarse_out,
                  held, own, shared, stack, chip, total, cross,
                  parts_a, pieces_a, summed_a, full_a, parts_b, pieces_b, summed_b, full_b,
                  k_sem, o_sem, a_send, a_recv, b_send, b_recv, c_send, c_recv,
                  ra_sems, rb_sems, m_send, m_recv, w_send, w_recv):
    s = lax.axis_index("src")
    t = lax.axis_index("tgt")
    core = lax.rem(s, 2)
    mate = flip(s, 1)
    across = flip(s, 2)
    half = rank // 2
    per = tiles // n_src

    def fetch(i):
        slot = lax.rem(i, slots)
        return pltpu.make_async_copy(
            kernel_hbm.at[pl.ds(pl.multiple_of(i * tile, tile), tile)], held.at[slot], k_sem.at[slot])

    for i in range(min(slots, tiles)):
        fetch(i).start()

    barrier = pltpu.get_barrier_semaphore()
    for mask in range(1, n_src):
        pl.semaphore_signal(barrier, inc=1, device_id={"src": flip(s, mask)}, device_id_type=MESH)
    for d in range(1, n_tgt):
        pl.semaphore_signal(barrier, inc=1, device_id={"tgt": lax.rem(t + d, n_tgt)}, device_id_type=MESH)
    pl.semaphore_wait(barrier, n_tgt + n_src - 2)

    mine = pl.multiple_of(half * core, half)
    theirs = pl.multiple_of(half * (1 - core), half)

    def share_pair(j):
        return remote(own.at[j, pl.ds(rank, rank)], shared.at[j, pl.ds(0, rank)],
                      a_send.at[0, j], a_recv.at[0, j], {"src": mate})

    def share_group(j):
        return remote(own.at[j, pl.ds(2 * rank + theirs, half)], shared.at[j, pl.ds(rank, half)],
                      a_send.at[1, j], a_recv.at[1, j], {"src": mate})

    def cross_chip(j):
        return remote(chip.at[0, j], chip.at[1, j], b_send.at[j], b_recv.at[j], {"src": across})

    def hand_over(j):
        return remote(chip.at[2, j], stack.at[j, pl.ds(2 * rank + mine, half)],
                      c_send.at[j], c_recv.at[j], {"src": mate})

    def move(mask, q):
        to = flip(s, mask)
        count = moved_rows(mask, rank)
        return remote(stack.at[to * per + q, pl.ds(0, count)], moved_out.at[mask - 1, q, pl.ds(0, count)],
                      m_send.at[mask - 1, q], m_recv.at[mask - 1, q], {"src": to})

    def save(j):
        return pltpu.make_async_copy(stack.at[j], stack_out.at[j], o_sem.at[j])

    total[...] = jnp.zeros_like(total)
    cross[...] = jnp.zeros_like(cross)

    def step(i, carry):
        @pl.when(i < tiles)
        def _():
            fetch(i).wait()
            own[i] = nt_dot(probes_ref[...], held[lax.rem(i, slots)])
            share_group(i).start()
            share_pair(i).start()

            @pl.when(i + slots < tiles)
            def _():
                fetch(i + slots).start()

        @pl.when(i >= 1)
        def _():
            j = i - 1
            share_group(j).wait_recv()
            chip[0, j] = own[j, pl.ds(2 * rank + mine, half)] + shared[j, rank:rank + half]
            cross_chip(j).start()
            share_pair(j).wait_recv()
            first = own[j, 0:rank]
            second = own[j, rank:2 * rank] + shared[j, 0:rank]
            both = jnp.concatenate([first, second], axis=0)
            stack[j, 0:2 * rank] = both
            high, low = split(both)
            total[...] += nt_dot(high, high)
            cross[...] += nt_dot(high, low)

        return carry

    lax.fori_loop(0, tiles + 1, step, 0)

    lower = Reduction(n_tgt, parts_a, pieces_a, summed_a, full_a, ra_sems)
    mixed = cross[...]
    lower.scatter(total[...] + (mixed + mixed.T))
    late = []
    for mask in (2, 3, 1) + tuple(range(4, n_src)):
        for q in range(per):
            if mask % 4 == 0:
                late.append((mask, q))
            else:
                move(mask, q).start()

    def group(j, carry):
        cross_chip(j).wait_recv()
        value = chip[0, j] + chip[1, j]
        chip[2, j] = value
        stack[j, pl.ds(2 * rank + mine, half)] = value
        hand_over(j).start()
        return carry

    early = tiles // 2
    lax.fori_loop(0, early, group, 0)
    lower.gather()
    lax.fori_loop(early, tiles, group, 0)

    def upper_gram(j, carry):
        hand_over(j).wait_recv()
        save(j).start()
        high, low = split(stack[j])
        top = high[2 * rank:]
        return carry + (nt_dot(top, high) + (nt_dot(top, low) + nt_dot(low[2 * rank:], high)))

    upper_value = lax.fori_loop(0, tiles, upper_gram, jnp.zeros((rank, 3 * rank), jnp.float32))
    for mask, q in late:
        move(mask, q).start()
    upper = Reduction(n_tgt, parts_b, pieces_b, summed_b, full_b, rb_sems)
    upper.scatter(upper_value)

    low_gram = lower.result()
    x0 = inverse_factor(low_gram[0:rank, 0:rank])
    c_pair = mmt(low_gram[rank:, 0:rank], x0)
    rest = low_gram[rank:, rank:] - mmt(c_pair, c_pair)
    upper.gather()
    x1 = inverse_factor(rest)
    mid_first = -mm(x1, mm(c_pair, x0))
    middle_out[:, 0:rank] = scale * mid_first
    middle_out[:, rank:] = scale * x1
    up_gram = upper.result()
    c_first = mmt(up_gram[:, 0:rank], x0)
    c_mid = mmt(up_gram[:, rank:2 * rank] - mmt(c_first, c_pair), x1)
    x2 = inverse_factor(up_gram[:, 2 * rank:] - mmt(c_first, c_first) - mmt(c_mid, c_mid))
    coarse_out[0, :, 0:rank] = -scale * mm(x2, mm(c_first, x0) + mm(c_mid, mid_first))
    coarse_out[0, :, rank:2 * rank] = -scale * mm(x2, mm(c_mid, x1))
    coarse_out[0, :, 2 * rank:] = scale * x2

    def tell(mask):
        return remote(coarse_out.at[0], coarse_out.at[mask], w_send.at[mask - 1], w_recv.at[mask - 1],
                      {"src": flip(s, mask)})

    for mask in range(1, n_src):
        tell(mask).start()

    lower.drain()
    upper.drain()

    def finish(j, carry):
        share_group(j).wait_send()
        share_pair(j).wait_send()
        cross_chip(j).wait_send()
        hand_over(j).wait_send()
        save(j).wait()
        return carry

    lax.fori_loop(0, tiles, finish, 0)
    for mask in range(1, n_src):
        for q in range(per):
            move(mask, q).wait()
    for mask in range(1, n_src):
        tell(mask).wait()


def gather(kernel, probes, tile, scale):
    n_src, n_tgt = lax.axis_size("src"), lax.axis_size("tgt")
    rows, cols = kernel.shape
    total_rank = probes.shape[0]
    rank = total_rank // 3
    tiles = rows // tile
    per = tiles // n_src
    slots = min(4, tiles)
    f32 = jnp.float32
    dma = pltpu.SemaphoreType.DMA
    low, up = 2 * rank, rank
    return pl.pallas_call(
        functools.partial(gather_kernel, n_src, n_tgt, tiles, tile, slots, rank, scale),
        out_shape=(jax.ShapeDtypeStruct((tiles, total_rank, tile), f32),
                   jax.ShapeDtypeStruct((n_src - 1, per, total_rank, tile), f32),
                   jax.ShapeDtypeStruct((rank, 2 * rank), f32),
                   jax.ShapeDtypeStruct((n_src, rank, total_rank), f32)),
        in_specs=[pl.BlockSpec(memory_space=pl.ANY), pl.BlockSpec(memory_space=pltpu.VMEM)],
        out_specs=(pl.BlockSpec(memory_space=pl.ANY), pl.BlockSpec(memory_space=pl.ANY),
                   pl.BlockSpec(memory_space=pltpu.VMEM), pl.BlockSpec(memory_space=pltpu.VMEM)),
        scratch_shapes=[
            pltpu.VMEM((slots, tile, cols), kernel.dtype),
            pltpu.VMEM((tiles, total_rank, tile), f32),
            pltpu.VMEM((tiles, rank + rank // 2, tile), f32),
            pltpu.VMEM((tiles, total_rank, tile), f32),
            pltpu.VMEM((3, tiles, rank // 2, tile), f32),
            pltpu.VMEM((low, low), f32),
            pltpu.VMEM((low, low), f32),
            pltpu.VMEM((n_tgt, low // n_tgt, low), f32),
            pltpu.VMEM((n_tgt - 1, low // n_tgt, low), f32),
            pltpu.VMEM((low // n_tgt, low), f32),
            pltpu.VMEM((n_tgt, low // n_tgt, low), f32),
            pltpu.VMEM((n_tgt, up // n_tgt, total_rank), f32),
            pltpu.VMEM((n_tgt - 1, up // n_tgt, total_rank), f32),
            pltpu.VMEM((up // n_tgt, total_rank), f32),
            pltpu.VMEM((n_tgt, up // n_tgt, total_rank), f32),
            dma((slots,)), dma((tiles,)),
            dma((2, tiles)), dma((2, tiles)), dma((tiles,)), dma((tiles,)), dma((tiles,)), dma((tiles,)),
            dma((4, n_tgt - 1)), dma((4, n_tgt - 1)),
            dma((n_src - 1, per)), dma((n_src - 1, per)), dma((n_src - 1,)), dma((n_src - 1,)),
        ],
        compiler_params=pltpu.CompilerParams(collective_id=0, has_side_effects=True),
        name="gather",
    )(kernel, probes)


def finish_kernel(n_src, tiles, tile, rank, stack_hbm, moved_hbm, middle_w, coarse_w, middle_ref, coarse_ref,
                  stack, moved, mine, middle, coarse, s_sem, m_sem, o_sem, mo_sem, co_sem):
    s = lax.axis_index("src")
    per = tiles // n_src

    def fetch(j):
        return pltpu.make_async_copy(stack_hbm.at[j, pl.ds(0, 2 * rank)], stack.at[j], s_sem.at[j])

    def fetch_mine(q):
        return pltpu.make_async_copy(stack_hbm.at[s * per + q], mine.at[q], o_sem.at[q])

    def fetch_moved(mask, q):
        count = moved_rows(mask, rank)
        return pltpu.make_async_copy(moved_hbm.at[mask - 1, q, pl.ds(0, count)],
                                     moved.at[mask - 1, q, pl.ds(0, count)], m_sem.at[mask - 1, q])

    for q in range(per):
        fetch_mine(q).start()
    for mask in range(1, n_src):
        for q in range(per):
            fetch_moved(mask, q).start()
    for j in range(tiles):
        fetch(j).start()

    def put_coarse(mask):
        return pltpu.make_async_copy(coarse.at[mask], coarse_ref.at[flip(s, mask)], co_sem.at[mask])

    def put_middle(j):
        return pltpu.make_async_copy(middle.at[j], middle_ref.at[0, :, pl.ds(j * tile, tile)], mo_sem.at[j])

    def product(weights, operand):
        w_high, w_low = split(weights)
        high, low = split(operand)
        count = weights.shape[0]
        both = jnp.dot(jnp.concatenate([w_high, w_low], axis=0), high, preferred_element_type=jnp.float32)
        return both[:count] + (both[count:] + jnp.dot(w_high, low, preferred_element_type=jnp.float32))

    for q in range(per):
        fetch_mine(q).wait()
    for mask in range(n_src):
        for q in range(per):
            if mask:
                fetch_moved(mask, q).wait()

            def rows(source, index):
                ref = moved.at[source - 1, q] if source else mine.at[q]
                return ref[index * rank:(index + 1) * rank]

            operand = jnp.concatenate(
                [rows(mask, 0), rows(mask - mask % 2, 1), rows(mask - mask % 4, 2)], axis=0)
            coarse[mask, :, 0, q * tile:(q + 1) * tile] = product(coarse_w[mask], operand)
        put_coarse(mask).start()
    for j in range(tiles):
        fetch(j).wait()
        middle[j] = product(middle_w[...], stack[j])
        put_middle(j).start()
    for mask in range(n_src):
        put_coarse(mask).wait()
    for j in range(tiles):
        put_middle(j).wait()


def finish(stack, moved, middle_w, coarse_w):
    n_src = lax.axis_size("src")
    tiles, total_rank, tile = stack.shape
    rank = total_rank // 3
    per = tiles // n_src
    f32 = jnp.float32
    dma = pltpu.SemaphoreType.DMA
    vmem = pl.BlockSpec(memory_space=pltpu.VMEM)
    hbm = pl.BlockSpec(memory_space=pl.ANY)
    return pl.pallas_call(
        functools.partial(finish_kernel, n_src, tiles, tile, rank),
        out_shape=(jax.ShapeDtypeStruct((1, rank, tiles * tile), f32),
                   jax.ShapeDtypeStruct((n_src, rank, 1, per * tile), f32)),
        in_specs=[hbm, hbm, vmem, vmem],
        out_specs=(hbm, hbm),
        scratch_shapes=[
            pltpu.VMEM((tiles, 2 * rank, tile), f32),
            pltpu.VMEM((n_src - 1, per, total_rank, tile), f32),
            pltpu.VMEM((per, total_rank, tile), f32),
            pltpu.VMEM((tiles, rank, tile), f32),
            pltpu.VMEM((n_src, rank, 1, per * tile), f32),
            dma((tiles,)), dma((n_src - 1, per)), dma((per,)), dma((tiles,)), dma((n_src,)),
        ],
        name="finish",
    )(stack, moved, middle_w, coarse_w)


def shards(kernel, probes):
    n_src, n_tgt = lax.axis_size("src"), lax.axis_size("tgt")
    rows = kernel.shape[0]
    scale = math.sqrt(rows * n_tgt)
    levels, rank, cols = probes.shape
    tile = min(512, rows // n_src)
    return finish(*gather(kernel, probes.reshape(levels * rank, cols), tile, scale))


def solution(mesh):
    placed = (P("tgt", "src"), P(None, None, "src"))
    return jax.shard_map(
        shards,
        mesh=mesh,
        in_specs=placed,
        out_specs=(P("src", None, "tgt"), P(None, None, "tgt", "src")),
        check_vma=False,
    )
```

```python
import functools
import math

import jax
import jax.numpy as jnp
from jax import lax
from jax.experimental import pallas as pl
from jax.experimental.pallas import tpu as pltpu
from jax.sharding import PartitionSpec as P

highest = lax.Precision.HIGHEST
MESH = pl.DeviceIdType.MESH


def nt_dot(a, b):
    return lax.dot_general(a, b, (((1,), (1,)), ((), ())), preferred_element_type=jnp.float32)


def split(value):
    high = value.astype(jnp.bfloat16)
    return high, (value - high.astype(jnp.float32)).astype(jnp.bfloat16)


def inverse_factor(a, chunk=4):
    n = a.shape[0]
    lanes = 2 * n
    m = jnp.concatenate([a, jnp.eye(n, dtype=a.dtype)], axis=1)
    blocks = [m[8 * r:8 * r + 8] for r in range(n // 8)]
    row_ids = lax.broadcasted_iota(jnp.int32, (8, lanes), 0)
    for start in range(0, n, chunk):
        top = start // 8
        cols = [{r: jnp.broadcast_to(blocks[r][:, start + q:start + q + 1], (8, lanes)) for r in range(top, n // 8)}
                for q in range(chunk)]
        for q in range(chunk):
            inner = (start + q) % 8
            pivot = jnp.broadcast_to(cols[q][top][inner:inner + 1], (8, lanes))
            inv = 1.0 / pivot
            row = jnp.broadcast_to(blocks[top][inner:inner + 1], (8, lanes))
            later = [jnp.broadcast_to(cols[p][top][inner:inner + 1], (8, lanes)) for p in range(q + 1, chunk)]
            row = row * inv
            later = [value * inv for value in later]
            for r in range(top, n // 8):
                mult = cols[q][r]
                if r == top:
                    mult = jnp.where(row_ids > inner, mult, 0.0)
                for p in range(q + 1, chunk):
                    cols[p][r] = cols[p][r] - mult * later[p - q - 1]
                blocks[r] = blocks[r] - mult * row
    m = jnp.concatenate(blocks, axis=0)
    r_ids = lax.broadcasted_iota(jnp.int32, (n, lanes), 0)
    c_ids = lax.broadcasted_iota(jnp.int32, (n, lanes), 1)
    pivots = jnp.sum(jnp.where(r_ids == c_ids, m, 0.0), axis=1, keepdims=True)
    return m[:, n:] * (1.0 / jnp.sqrt(pivots))


def mm(a, b):
    return lax.dot_general(a, b, (((1,), (0,)), ((), ())), precision=highest, preferred_element_type=jnp.float32)


def mmt(a, b):
    return lax.dot_general(a, b, (((1,), (1,)), ((), ())), precision=highest, preferred_element_type=jnp.float32)


def flip(index, mask):
    result = 0
    place = 1
    while place <= mask:
        bit = lax.rem(index // place, 2)
        result = result + place * ((1 - bit) if mask & place else bit)
        place *= 2
    return result + (index // place) * place


def remote(src, dst, send, recv, device):
    return pltpu.make_async_remote_copy(
        src_ref=src, dst_ref=dst, send_sem=send, recv_sem=recv, device_id=device, device_id_type=MESH)


class Reduction:
    def __init__(self, n, parts, pieces, summed, full, sems):
        self.n, self.parts, self.pieces, self.summed, self.full = n, parts, pieces, summed, full
        self.r_send, self.r_recv, self.g_send, self.g_recv = (sems.at[k] for k in range(4))
        self.t = lax.axis_index("tgt")

    def scatter(self, value):
        rows = value.shape[0] // self.n
        for p in range(self.n):
            self.parts[p] = value[p * rows:(p + 1) * rows]
        self.sent = []
        for d in range(1, self.n):
            to = lax.rem(self.t + d, self.n)
            self.sent.append(remote(self.parts.at[to], self.pieces.at[d - 1],
                                    self.r_send.at[d - 1], self.r_recv.at[d - 1], {"tgt": to}))
            self.sent[-1].start()

    def gather(self):
        value = self.parts[self.t]
        for d in range(1, self.n):
            self.sent[d - 1].wait_recv()
            value = value + self.pieces[d - 1]
        self.summed[...] = value
        self.full[self.t] = value
        for d in range(1, self.n):
            to = lax.rem(self.t + d, self.n)
            self.sent.append(remote(self.summed, self.full.at[self.t],
                                    self.g_send.at[d - 1], self.g_recv.at[d - 1], {"tgt": to}))
            self.sent[-1].start()

    def result(self):
        for d in range(1, self.n):
            origin = lax.rem(self.t + self.n - d, self.n)
            remote(self.summed, self.full.at[origin], self.g_send.at[d - 1], self.g_recv.at[d - 1],
                   {"tgt": origin}).wait_recv()
        return jnp.concatenate([self.full[p] for p in range(self.n)], axis=0)

    def drain(self):
        for copy in self.sent:
            copy.wait_send()


def moved_rows(mask, rank):
    return rank * (3 if mask % 4 == 0 else 2 if mask % 2 == 0 else 1)


def gather_kernel(n_src, n_tgt, tiles, tile, slots, rank, scale,
                  kernel_hbm, probes_ref, stack_out, moved_out, middle_out, coarse_out,
                  held, own, shared, stack, chip, total,
                  parts_a, pieces_a, summed_a, full_a, parts_b, pieces_b, summed_b, full_b,
                  k_sem, o_sem, a_send, a_recv, b_send, b_recv, c_send, c_recv,
                  ra_sems, rb_sems, m_send, m_recv, w_send, w_recv):
    s = lax.axis_index("src")
    t = lax.axis_index("tgt")
    core = lax.rem(s, 2)
    mate = flip(s, 1)
    across = flip(s, 2)
    half = rank // 2
    per = tiles // n_src

    def fetch(i):
        slot = lax.rem(i, slots)
        return pltpu.make_async_copy(
            kernel_hbm.at[pl.ds(pl.multiple_of(i * tile, tile), tile)], held.at[slot], k_sem.at[slot])

    for i in range(min(slots, tiles)):
        fetch(i).start()

    barrier = pltpu.get_barrier_semaphore()
    for mask in range(1, n_src):
        pl.semaphore_signal(barrier, inc=1, device_id={"src": flip(s, mask)}, device_id_type=MESH)
    for d in range(1, n_tgt):
        pl.semaphore_signal(barrier, inc=1, device_id={"tgt": lax.rem(t + d, n_tgt)}, device_id_type=MESH)
    pl.semaphore_wait(barrier, n_tgt + n_src - 2)

    mine = pl.multiple_of(half * core, half)
    theirs = pl.multiple_of(half * (1 - core), half)

    def share_pair(j):
        return remote(own.at[j, pl.ds(rank, rank)], shared.at[j, pl.ds(0, rank)],
                      a_send.at[0, j], a_recv.at[0, j], {"src": mate})

    def share_group(j):
        return remote(own.at[j, pl.ds(2 * rank + theirs, half)], shared.at[j, pl.ds(rank, half)],
                      a_send.at[1, j], a_recv.at[1, j], {"src": mate})

    def cross_chip(j):
        return remote(chip.at[0, j], chip.at[1, j], b_send.at[j], b_recv.at[j], {"src": across})

    def hand_over(j):
        return remote(chip.at[2, j], stack.at[j, pl.ds(2 * rank + mine, half)],
                      c_send.at[j], c_recv.at[j], {"src": mate})

    def move(mask, q):
        to = flip(s, mask)
        count = moved_rows(mask, rank)
        return remote(stack.at[to * per + q, pl.ds(0, count)], moved_out.at[mask - 1, q, pl.ds(0, count)],
                      m_send.at[mask - 1, q], m_recv.at[mask - 1, q], {"src": to})

    def save(j):
        return pltpu.make_async_copy(stack.at[j], stack_out.at[j], o_sem.at[j])

    total[...] = jnp.zeros_like(total)

    def step(i, carry):
        @pl.when(i < tiles)
        def _():
            fetch(i).wait()
            own[i] = nt_dot(probes_ref[...], held[lax.rem(i, slots)])
            share_group(i).start()
            share_pair(i).start()

            @pl.when(i + slots < tiles)
            def _():
                fetch(i + slots).start()

        @pl.when(i >= 1)
        def _():
            j = i - 1
            share_group(j).wait_recv()
            chip[0, j] = own[j, pl.ds(2 * rank + mine, half)] + shared[j, rank:rank + half]
            cross_chip(j).start()
            share_pair(j).wait_recv()
            first = own[j, 0:rank]
            second = own[j, rank:2 * rank] + shared[j, 0:rank]
            both = jnp.concatenate([first, second], axis=0)
            stack[j, 0:2 * rank] = both
            high, low = split(both)
            total[...] += nt_dot(high, jnp.concatenate([high, low], axis=0))

        return carry

    lax.fori_loop(0, tiles + 1, step, 0)

    lower = Reduction(n_tgt, parts_a, pieces_a, summed_a, full_a, ra_sems)
    mixed = total[:, 2 * rank:]
    lower.scatter(total[:, 0:2 * rank] + (mixed + mixed.T))
    late = []
    for mask in (2, 3, 1) + tuple(range(4, n_src)):
        for q in range(per):
            if mask % 4 == 0:
                late.append((mask, q))
            else:
                move(mask, q).start()

    def group(j, carry):
        cross_chip(j).wait_recv()
        value = chip[0, j] + chip[1, j]
        chip[2, j] = value
        stack[j, pl.ds(2 * rank + mine, half)] = value
        hand_over(j).start()
        return carry

    early = tiles // 2
    lax.fori_loop(0, early, group, 0)
    lower.gather()
    lax.fori_loop(early, tiles, group, 0)

    def upper_gram(j, carry):
        hand_over(j).wait_recv()
        save(j).start()
        high, low = split(stack[j])
        top = high[2 * rank:]
        return carry + (nt_dot(top, high) + (nt_dot(top, low) + nt_dot(low[2 * rank:], high)))

    upper_value = lax.fori_loop(0, tiles, upper_gram, jnp.zeros((rank, 3 * rank), jnp.float32))
    for mask, q in late:
        move(mask, q).start()
    upper = Reduction(n_tgt, parts_b, pieces_b, summed_b, full_b, rb_sems)
    upper.scatter(upper_value)

    low_gram = lower.result()
    x0 = inverse_factor(low_gram[0:rank, 0:rank])
    c_pair = mmt(low_gram[rank:, 0:rank], x0)
    rest = low_gram[rank:, rank:] - mmt(c_pair, c_pair)
    upper.gather()
    x1 = inverse_factor(rest)
    mid_first = -mm(x1, mm(c_pair, x0))
    middle_out[:, 0:rank] = scale * mid_first
    middle_out[:, rank:] = scale * x1
    up_gram = upper.result()
    c_first = mmt(up_gram[:, 0:rank], x0)
    c_mid = mmt(up_gram[:, rank:2 * rank] - mmt(c_first, c_pair), x1)
    x2 = inverse_factor(up_gram[:, 2 * rank:] - mmt(c_first, c_first) - mmt(c_mid, c_mid))
    coarse_out[0, :, 0:rank] = -scale * mm(x2, mm(c_first, x0) + mm(c_mid, mid_first))
    coarse_out[0, :, rank:2 * rank] = -scale * mm(x2, mm(c_mid, x1))
    coarse_out[0, :, 2 * rank:] = scale * x2

    def tell(mask):
        return remote(coarse_out.at[0], coarse_out.at[mask], w_send.at[mask - 1], w_recv.at[mask - 1],
                      {"src": flip(s, mask)})

    for mask in range(1, n_src):
        tell(mask).start()

    lower.drain()
    upper.drain()

    def finish(j, carry):
        share_group(j).wait_send()
        share_pair(j).wait_send()
        cross_chip(j).wait_send()
        hand_over(j).wait_send()
        save(j).wait()
        return carry

    lax.fori_loop(0, tiles, finish, 0)
    for mask in range(1, n_src):
        for q in range(per):
            move(mask, q).wait()
    for mask in range(1, n_src):
        tell(mask).wait()


def gather(kernel, probes, tile, scale):
    n_src, n_tgt = lax.axis_size("src"), lax.axis_size("tgt")
    rows, cols = kernel.shape
    total_rank = probes.shape[0]
    rank = total_rank // 3
    tiles = rows // tile
    per = tiles // n_src
    slots = min(4, tiles)
    f32 = jnp.float32
    dma = pltpu.SemaphoreType.DMA
    low, up = 2 * rank, rank
    return pl.pallas_call(
        functools.partial(gather_kernel, n_src, n_tgt, tiles, tile, slots, rank, scale),
        out_shape=(jax.ShapeDtypeStruct((tiles, total_rank, tile), f32),
                   jax.ShapeDtypeStruct((n_src - 1, per, total_rank, tile), f32),
                   jax.ShapeDtypeStruct((rank, 2 * rank), f32),
                   jax.ShapeDtypeStruct((n_src, rank, total_rank), f32)),
        in_specs=[pl.BlockSpec(memory_space=pl.ANY), pl.BlockSpec(memory_space=pltpu.VMEM)],
        out_specs=(pl.BlockSpec(memory_space=pl.ANY), pl.BlockSpec(memory_space=pl.ANY),
                   pl.BlockSpec(memory_space=pltpu.VMEM), pl.BlockSpec(memory_space=pltpu.VMEM)),
        scratch_shapes=[
            pltpu.VMEM((slots, tile, cols), kernel.dtype),
            pltpu.VMEM((tiles, total_rank, tile), f32),
            pltpu.VMEM((tiles, rank + rank // 2, tile), f32),
            pltpu.VMEM((tiles, total_rank, tile), f32),
            pltpu.VMEM((3, tiles, rank // 2, tile), f32),
            pltpu.VMEM((low, 2 * low), f32),
            pltpu.VMEM((n_tgt, low // n_tgt, low), f32),
            pltpu.VMEM((n_tgt - 1, low // n_tgt, low), f32),
            pltpu.VMEM((low // n_tgt, low), f32),
            pltpu.VMEM((n_tgt, low // n_tgt, low), f32),
            pltpu.VMEM((n_tgt, up // n_tgt, total_rank), f32),
            pltpu.VMEM((n_tgt - 1, up // n_tgt, total_rank), f32),
            pltpu.VMEM((up // n_tgt, total_rank), f32),
            pltpu.VMEM((n_tgt, up // n_tgt, total_rank), f32),
            dma((slots,)), dma((tiles,)),
            dma((2, tiles)), dma((2, tiles)), dma((tiles,)), dma((tiles,)), dma((tiles,)), dma((tiles,)),
            dma((4, n_tgt - 1)), dma((4, n_tgt - 1)),
            dma((n_src - 1, per)), dma((n_src - 1, per)), dma((n_src - 1,)), dma((n_src - 1,)),
        ],
        compiler_params=pltpu.CompilerParams(collective_id=0, has_side_effects=True),
        name="gather",
    )(kernel, probes)


def finish_kernel(n_src, tiles, tile, rank, stack_hbm, moved_hbm, middle_w, coarse_w, middle_ref, coarse_ref,
                  stack, moved, mine, middle, coarse, s_sem, m_sem, o_sem, mo_sem, co_sem):
    s = lax.axis_index("src")
    per = tiles // n_src

    def fetch(j):
        return pltpu.make_async_copy(stack_hbm.at[j, pl.ds(0, 2 * rank)], stack.at[j], s_sem.at[j])

    def fetch_mine(q):
        return pltpu.make_async_copy(stack_hbm.at[s * per + q], mine.at[q], o_sem.at[q])

    def fetch_moved(mask, q):
        count = moved_rows(mask, rank)
        return pltpu.make_async_copy(moved_hbm.at[mask - 1, q, pl.ds(0, count)],
                                     moved.at[mask - 1, q, pl.ds(0, count)], m_sem.at[mask - 1, q])

    for q in range(per):
        fetch_mine(q).start()
    for mask in range(1, n_src):
        for q in range(per):
            fetch_moved(mask, q).start()
    for j in range(tiles):
        fetch(j).start()

    def put_coarse(mask):
        return pltpu.make_async_copy(coarse.at[mask], coarse_ref.at[flip(s, mask)], co_sem.at[mask])

    def put_middle(j):
        return pltpu.make_async_copy(middle.at[j], middle_ref.at[0, :, pl.ds(j * tile, tile)], mo_sem.at[j])

    def product(weights, operand):
        w_high, w_low = split(weights)
        high, low = split(operand)
        count = weights.shape[0]
        both = jnp.dot(jnp.concatenate([w_high, w_low], axis=0), high, preferred_element_type=jnp.float32)
        return both[:count] + (both[count:] + jnp.dot(w_high, low, preferred_element_type=jnp.float32))

    for q in range(per):
        fetch_mine(q).wait()
    for mask in range(n_src):
        for q in range(per):
            if mask:
                fetch_moved(mask, q).wait()

            def rows(source, index):
                ref = moved.at[source - 1, q] if source else mine.at[q]
                return ref[index * rank:(index + 1) * rank]

            operand = jnp.concatenate(
                [rows(mask, 0), rows(mask - mask % 2, 1), rows(mask - mask % 4, 2)], axis=0)
            coarse[mask, :, 0, q * tile:(q + 1) * tile] = product(coarse_w[mask], operand)
        put_coarse(mask).start()
    w_high, w_low = split(middle_w[...])
    wide = jnp.concatenate([jnp.concatenate([w_high, w_high], axis=1),
                            jnp.concatenate([w_low, jnp.zeros_like(w_low)], axis=1)], axis=0)
    for j in range(tiles):
        fetch(j).wait()
        value = jnp.dot(wide, jnp.concatenate(split(stack[j]), axis=0), preferred_element_type=jnp.float32)
        middle[j] = value[0:rank] + value[rank:]
        put_middle(j).start()
    for mask in range(n_src):
        put_coarse(mask).wait()
    for j in range(tiles):
        put_middle(j).wait()


def finish(stack, moved, middle_w, coarse_w):
    n_src = lax.axis_size("src")
    tiles, total_rank, tile = stack.shape
    rank = total_rank // 3
    per = tiles // n_src
    f32 = jnp.float32
    dma = pltpu.SemaphoreType.DMA
    vmem = pl.BlockSpec(memory_space=pltpu.VMEM)
    hbm = pl.BlockSpec(memory_space=pl.ANY)
    return pl.pallas_call(
        functools.partial(finish_kernel, n_src, tiles, tile, rank),
        out_shape=(jax.ShapeDtypeStruct((1, rank, tiles * tile), f32),
                   jax.ShapeDtypeStruct((n_src, rank, 1, per * tile), f32)),
        in_specs=[hbm, hbm, vmem, vmem],
        out_specs=(hbm, hbm),
        scratch_shapes=[
            pltpu.VMEM((tiles, 2 * rank, tile), f32),
            pltpu.VMEM((n_src - 1, per, total_rank, tile), f32),
            pltpu.VMEM((per, total_rank, tile), f32),
            pltpu.VMEM((tiles, rank, tile), f32),
            pltpu.VMEM((n_src, rank, 1, per * tile), f32),
            dma((tiles,)), dma((n_src - 1, per)), dma((per,)), dma((tiles,)), dma((n_src,)),
        ],
        name="finish",
    )(stack, moved, middle_w, coarse_w)


def shards(kernel, probes):
    n_src, n_tgt = lax.axis_size("src"), lax.axis_size("tgt")
    rows = kernel.shape[0]
    scale = math.sqrt(rows * n_tgt)
    levels, rank, cols = probes.shape
    tile = min(512, rows // n_src)
    return finish(*gather(kernel, probes.reshape(levels * rank, cols), tile, scale))


def solution(mesh):
    placed = (P("tgt", "src"), P(None, None, "src"))
    return jax.shard_map(
        shards,
        mesh=mesh,
        in_specs=placed,
        out_specs=(P("src", None, "tgt"), P(None, None, "tgt", "src")),
        check_vma=False,
    )
```
